32 devices in a mesh: group: 2 (over x), seq: 16 (over z, y, core).
Axes of the slice: x: 2, y: 2, z: 4, core: 2. Of those that a mesh axis runs over, the one named last changes fastest.
Arguments:
- query_rows: bfloat16 [16384, 2048], P(('group', 'seq')), parts along dimension 0, may hold values from -5 to 5
- key_rows: bfloat16 [16384, 2048], P(('group', 'seq')), parts along dimension 0, may hold values from -5 to 5
- value_rows: bfloat16 [16384, 2048], P(('group', 'seq')), parts along dimension 0, may hold values from -5 to 5
Outputs:
- mixed_heads: bfloat16 [16384, 2048], P(('group', 'seq')), parts along dimension 0
The draws below stay inside these ranges and needn't reach their ends.
There are 2 independent parts, one for each index of `group`. The reference program is written for one: setup_inputs(seed, part) draws one part's arguments, and reference() takes and returns one part's arrays. A program takes and returns all parts, laid end to end along the dimension named above; each array names one. Nothing has to cross between parts.
All inputs are finite; a program needn't handle non-finite values.
Results may differ from the reference program's by a relative error of at most 0.0034.
Values may be sent and summed in bfloat16 or wider, within the bound.
A program may use at most 192 MiB of HBM per device.

```python
import math
import jax
import jax.numpy as jnp
from jax import lax

H = 16
DH = 128
WINDOW = 2048
BLOCK = 128
HD = 2048
TOKENS = 8192


def draw_query_rows(key, part):
    result_rows = jnp.clip(jax.random.normal(jax.random.fold_in(key, 1), (TOKENS, HD), jnp.float32), -5.0, 5.0)
    return result_rows.astype(jnp.bfloat16)


def draw_key_rows(key, part):
    result_rows = jnp.clip(jax.random.normal(jax.random.fold_in(key, 2), (TOKENS, HD), jnp.float32), -5.0, 5.0)
    return result_rows.astype(jnp.bfloat16)


def block_levels(stream_key, shape, split, low, high):
    def one(dim, shards_of):
        draws = jax.random.uniform(jax.random.fold_in(jax.random.fold_in(stream_key, 6), dim), (shards_of,), jnp.float32, low / len(split), high / len(split))
        return jnp.repeat(jnp.exp(draws), shape[dim] // shards_of).reshape((-1,) + (1,) * (len(shape) - dim - 1))

    level = one(*split[0])
    for cut in split[1:]:
        level = level * one(*cut)
    return level


def gaussian(rng, dims, width, limit, cuts=(), kind=jnp.bfloat16):
    values = jax.random.normal(rng, dims, jnp.float32) * width
    if len(cuts) > 0:
        values = block_levels(rng, dims, cuts, -0.22, 0.18) * values
    return jnp.clip(values, min=-limit, max=limit).astype(kind)


def setup_inputs(seed: int = 0, part: int = 0) -> dict:
    keys = jax.random.split(jax.random.key(seed), 4)
    part_keys = jax.random.split(jax.random.fold_in(keys[3], part), 4)
    return {
        "query_rows": draw_query_rows(jax.random.fold_in(jax.random.fold_in(keys[3], part), 71), part),
        "key_rows": draw_key_rows(jax.random.fold_in(jax.random.fold_in(keys[3], part), 71), part),
        "value_rows": gaussian(part_keys[2], (TOKENS, HD), 1.0, 5.0, ((0, 16),)),
    }


EPSILON = 1e-06

def head_norm(vectors):
    return vectors * lax.rsqrt(lax.optimization_barrier(jnp.mean(vectors * vectors, axis=-1, keepdims=True)) + EPSILON)

def linear_branch(query_rows, key_rows, value_rows):
    block_count = TOKENS // BLOCK
    q_blocks = query_rows.reshape(block_count, BLOCK, H, DH)
    k_blocks = key_rows.reshape(block_count, BLOCK, H, DH)
    v_blocks = value_rows.reshape(block_count, BLOCK, H, DH)
    causal = jnp.arange(BLOCK)[:, None] >= jnp.arange(BLOCK)[None, :]

    def advance(state_sum, pieces):
        query_block, key_block, value_block = pieces
        query_wide = query_block.astype(jnp.float32)
        key_wide = key_block.astype(jnp.float32)
        value_wide = value_block.astype(jnp.float32)
        scores = jnp.einsum('qhd,khd->hqk', query_wide, key_wide)
        scores = jnp.where(causal[None], scores, 0.0).astype(jnp.bfloat16)
        inner_term = jnp.einsum('hqk,khd->qhd', scores.astype(jnp.float32), value_wide)
        cross_term = jnp.einsum('qhd,hde->qhe', query_wide, state_sum, precision=lax.Precision.HIGHEST)
        state_sum = state_sum + jnp.einsum('khd,khe->hde', key_wide, value_wide)
        return (state_sum, cross_term + inner_term)
    start_state = jnp.zeros((H, DH, DH), jnp.float32)
    final_state, linear = lax.scan(advance, start_state, (q_blocks, k_blocks, v_blocks))
    return linear.reshape(TOKENS, H, DH)

def window_branch(query_rows, key_rows, value_rows):
    query_span = min(512, TOKENS)
    block_count = TOKENS // query_span
    padded_keys = jnp.concatenate([jnp.zeros((WINDOW, H * DH), jnp.bfloat16), key_rows], axis=0)
    padded_values = jnp.concatenate([jnp.zeros((WINDOW, H * DH), jnp.bfloat16), value_rows], axis=0)
    score_scale = 1.0 / math.sqrt(DH)

    def one_block(block_index):
        block_start = (block_index * query_span).astype(jnp.int32)
        query_block = lax.dynamic_slice_in_dim(query_rows, block_start, query_span, 0)
        query_block = query_block.reshape(query_span, H, DH).astype(jnp.float32)
        key_block = lax.dynamic_slice_in_dim(padded_keys, block_start, WINDOW + query_span, 0)
        key_block = key_block.reshape(WINDOW + query_span, H, DH).astype(jnp.float32)
        value_block = lax.dynamic_slice_in_dim(padded_values, block_start, WINDOW + query_span, 0)
        value_block = value_block.reshape(WINDOW + query_span, H, DH).astype(jnp.float32)
        query_pos = block_start + jnp.arange(query_span, dtype=jnp.int32)
        key_pos = block_start - WINDOW + jnp.arange(WINDOW + query_span, dtype=jnp.int32)
        allowed = (key_pos[None, :] <= query_pos[:, None]) & (key_pos[None, :] > query_pos[:, None] - WINDOW) & (key_pos[None, :] >= 0)
        scores = jnp.einsum('qhd,khd->hqk', query_block, key_block) * score_scale
        scores = jnp.where(allowed[None], scores, -1e+30)
        row_peak = lax.optimization_barrier(jnp.max(scores, axis=-1, keepdims=True))
        weights = jnp.exp(scores - row_peak)
        weights = weights / lax.optimization_barrier(jnp.sum(weights, axis=-1, keepdims=True))
        weights = weights.astype(jnp.bfloat16)
        return jnp.einsum('hqk,khd->qhd', weights.astype(jnp.float32), value_block)
    blocks = lax.map(one_block, jnp.arange(block_count, dtype=jnp.int32))
    return blocks.reshape(TOKENS, H, DH)

def reference(query_rows, key_rows, value_rows):
    linear = linear_branch(query_rows, key_rows, value_rows)
    window = window_branch(query_rows, key_rows, value_rows)
    mixed_out = head_norm(linear) + head_norm(window)
    return mixed_out.reshape(TOKENS, H * DH).astype(jnp.bfloat16)
```

```python
import functools
import math

import jax
import jax.numpy as jnp
from jax import lax
from jax.experimental import pallas as pl
from jax.experimental.pallas import tpu as pltpu
from jax.sharding import PartitionSpec as P

H = 16
DH = 128
WINDOW = 2048
TILE = 256
EPSILON = 1e-06
EXP_SCALE = math.log2(math.e) / math.sqrt(DH)
NEG = -1e30
F32 = jnp.float32
BF16 = jnp.bfloat16
MESH = pl.DeviceIdType.MESH


def dot_nt(a, b):
    return lax.dot_general(a, b, (((1,), (1,)), ((), ())), preferred_element_type=F32)


def dot_tn(a, b):
    return lax.dot_general(a, b, (((0,), (0,)), ((), ())), preferred_element_type=F32)


def dot_nn(a, b):
    return jnp.dot(a, b, preferred_element_type=F32)


def times_state(q, state):
    high = state.astype(BF16)
    low = (state - high.astype(F32)).astype(BF16)
    both = dot_nn(q, jnp.concatenate([high, low], axis=1))
    return both[:, :DH] + both[:, DH:]


def head_norm(x):
    return x * lax.rsqrt(jnp.mean(x * x, axis=-1, keepdims=True) + EPSILON)


def kernel(
    layer, layers, rows,
    q_hbm, k_hbm, v_hbm, out_hbm,
    qb, kb, vb, kh, vh, ob, o_acc, m_acc, l_acc, lin_acc, total, state_in, state_out,
    own_sem, a_send, a_recv, z_send, z_recv, s_send, s_recv, o_own, o_send, o_recv,
):
    me = lax.axis_index("seq")
    place = lax.rem(me, layer)
    level = me // layer
    base = level * layer
    heads = H // layer
    span = layer * rows
    tiles = span // TILE
    has_before = level > 0
    has_after = level < layers - 1

    def peer(d):
        return base + lax.rem(place + d, layer)

    barrier = pltpu.get_barrier_semaphore()
    for d in range(1, layer):
        pl.semaphore_signal(barrier, inc=1, device_id={"seq": peer(d)}, device_id_type=MESH)

    @pl.when(has_before)
    def _():
        pl.semaphore_signal(barrier, inc=1, device_id={"seq": me - layer}, device_id_type=MESH)

    @pl.when(has_after)
    def _():
        pl.semaphore_signal(barrier, inc=1, device_id={"seq": me + layer}, device_id_type=MESH)

    ends = has_before.astype(jnp.int32) + has_after.astype(jnp.int32)
    pl.semaphore_wait(barrier, layer - 1 + ends)

    sources = (k_hbm, v_hbm, q_hbm)
    targets = (kb, vb, qb)

    def columns(owner, c):
        return pl.ds(pl.multiple_of((owner * heads + c) * DH, DH), DH)

    my_rows = pl.ds(pl.multiple_of(place * rows, rows), rows)

    def own_copy(c, t):
        return pltpu.make_async_copy(
            sources[t].at[:, columns(place, c)], targets[t].at[c, my_rows, :], own_sem.at[c, t]
        )

    def peer_copy(c, d, t):
        return pltpu.make_async_remote_copy(
            src_ref=sources[t].at[:, columns(lax.rem(place + d, layer), c)],
            dst_ref=targets[t].at[c, my_rows, :],
            send_sem=a_send.at[c, d - 1, t],
            recv_sem=a_recv.at[c, d - 1, t],
            device_id={"seq": peer(d)},
            device_id_type=MESH,
        )

    def next_copy(c, t):
        return pltpu.make_async_remote_copy(
            src_ref=(kb, vb)[t].at[c],
            dst_ref=(kh, vh)[t].at[c],
            send_sem=z_send.at[c, t],
            recv_sem=z_recv.at[c, t],
            device_id={"seq": me + layer},
            device_id_type=MESH,
        )

    def state_copy(c):
        return pltpu.make_async_remote_copy(
            src_ref=state_out.at[c],
            dst_ref=state_in.at[c],
            send_sem=s_send.at[c],
            recv_sem=s_recv.at[c],
            device_id={"seq": me + layer},
            device_id_type=MESH,
        )

    def out_copy(c, d):
        to_rows = pl.ds(pl.multiple_of(lax.rem(place + d, layer) * rows, rows), rows)
        return pltpu.make_async_remote_copy(
            src_ref=ob.at[c, to_rows, :],
            dst_ref=out_hbm.at[:, columns(place, c)],
            send_sem=o_send.at[c, d - 1],
            recv_sem=o_recv.at[c, d - 1],
            device_id={"seq": peer(d)},
            device_id_type=MESH,
        )

    def out_own(c):
        return pltpu.make_async_copy(
            ob.at[c, my_rows, :], out_hbm.at[:, columns(place, c)], o_own.at[c]
        )

    def start_chunk(c):
        for t in range(3):
            for d in range(layer - 1, 0, -1):
                peer_copy(c, d, t).start()
            own_copy(c, t).start()

    def wait_tensor(c, t):
        own_copy(c, t).wait()
        for d in range(1, layer):
            peer_copy(c, d, t).wait_recv()

    row_id = lax.broadcasted_iota(jnp.int32, (TILE, TILE), 0)
    col_id = lax.broadcasted_iota(jnp.int32, (TILE, TILE), 1)

    def part_softmax(q, k_full, v_full, s_diag, v_diag):
        peak = jnp.max(s_diag, axis=-1, keepdims=True)
        if k_full is not None:
            s_full = dot_nt(q, k_full)
            peak = jnp.maximum(peak, jnp.max(s_full, axis=-1, keepdims=True))
        p_diag = jnp.exp2((s_diag - peak) * EXP_SCALE)
        mass = jnp.sum(p_diag, axis=-1, keepdims=True)
        acc = dot_nn(p_diag.astype(BF16), v_diag)
        if k_full is not None:
            p_full = jnp.exp2((s_full - peak) * EXP_SCALE)
            mass = mass + jnp.sum(p_full, axis=-1, keepdims=True)
            acc = acc + dot_nn(p_full.astype(BF16), v_full)
        return peak, mass, acc

    def local_part(c, slot):
        causal = row_id >= col_id
        state = jnp.zeros((DH, DH), F32)
        for i in range(tiles):
            here = slice(i * TILE, (i + 1) * TILE)
            q, k, v = qb[c, here, :], kb[c, here, :], vb[c, here, :]
            scores = dot_nt(q, k)
            lin = dot_nn(jnp.where(causal, scores, 0.0).astype(BF16), v)
            if i > 0:
                lin = lin + times_state(q, state)
            lin_acc[slot, here, :] = lin
            state = state + dot_tn(k, v)
            k_full = kb[c, : i * TILE, :] if i > 0 else None
            v_full = vb[c, : i * TILE, :] if i > 0 else None
            peak, mass, acc = part_softmax(q, k_full, v_full, jnp.where(causal, scores, NEG), v)
            o_acc[slot, here, :] = acc
            m_acc[slot, here, :] = jnp.broadcast_to(peak, (TILE, DH))
            l_acc[slot, here, :] = jnp.broadcast_to(mass, (TILE, DH))
        total[c] = state

    def halo_part(c, slot):
        inside = col_id > row_id
        state = state_in[c]
        for i in range(tiles):
            here = slice(i * TILE, (i + 1) * TILE)
            q, k, v = qb[c, here, :], kh[c, here, :], vh[c, here, :]
            scores = jnp.where(inside, dot_nt(q, k), NEG)
            lin_acc[slot, here, :] += times_state(q, state)
            k_full = kh[c, (i + 1) * TILE :, :] if i < tiles - 1 else None
            v_full = vh[c, (i + 1) * TILE :, :] if i < tiles - 1 else None
            peak, mass, acc = part_softmax(q, k_full, v_full, scores, v)
            before = m_acc[slot, here, :]
            both = jnp.maximum(before, peak)
            keep = jnp.exp2((before - both) * EXP_SCALE)
            take = jnp.exp2((peak - both) * EXP_SCALE)
            o_acc[slot, here, :] = o_acc[slot, here, :] * keep + acc * take
            l_acc[slot, here, :] = l_acc[slot, here, :] * keep + mass * take

    start_chunk(0)
    if heads > 1:
        start_chunk(1)

    def step(c, _):
        @pl.when(c < heads)
        def _():
            wait_tensor(c, 0)
            wait_tensor(c, 1)

            @pl.when(has_after)
            def _():
                next_copy(c, 0).start()
                next_copy(c, 1).start()

            @pl.when(c + 2 < heads)
            def _():
                start_chunk(c + 2)

            wait_tensor(c, 2)
            local_part(c, lax.rem(c, 2))

        @pl.when(c > 0)
        def _():
            h = c - 1
            slot = lax.rem(h, 2)

            @pl.when(has_before)
            def _():
                state_copy(h).wait_recv()

            @pl.when(has_after)
            def _():
                @pl.when(has_before)
                def _():
                    state_out[h] = state_in[h] + total[h]

                @pl.when(level == 0)
                def _():
                    state_out[h] = total[h]

                state_copy(h).start()

            @pl.when(has_before)
            def _():
                next_copy(h, 0).wait_recv()
                next_copy(h, 1).wait_recv()
                halo_part(h, slot)

            def finish(i, _):
                here = pl.ds(pl.multiple_of(i * TILE, TILE), TILE)
                win = o_acc[slot, here, :] / l_acc[slot, here, :]
                ob[h, here, :] = (head_norm(lin_acc[slot, here, :]) + head_norm(win)).astype(BF16)
                return 0

            lax.fori_loop(0, tiles, finish, 0)
            for d in range(1, layer):
                out_copy(h, d).start()
            out_own(h).start()

        return 0

    lax.fori_loop(0, heads + 1, step, 0)

    def drain(c, _):
        for d in range(1, layer):
            for t in range(3):
                peer_copy(c, d, t).wait_send()
            out_copy(c, d).wait_send()
            out_copy(c, d).wait_recv()
        out_own(c).wait()

        @pl.when(has_after)
        def _():
            next_copy(c, 0).wait_send()
            next_copy(c, 1).wait_send()
            state_copy(c).wait_send()

        return 0

    lax.fori_loop(0, heads, drain, 0)


def per_device(query_rows, key_rows, value_rows):
    rows = query_rows.shape[0]
    layer = WINDOW // rows
    layers = lax.axis_size("seq") // layer
    heads = H // layer
    span = layer * rows
    dma = pltpu.SemaphoreType.DMA
    return pl.pallas_call(
        functools.partial(kernel, layer, layers, rows),
        out_shape=jax.ShapeDtypeStruct(query_rows.shape, BF16),
        in_specs=[pl.BlockSpec(memory_space=pl.ANY)] * 3,
        out_specs=pl.BlockSpec(memory_space=pl.ANY),
        scratch_shapes=[pltpu.VMEM((heads, span, DH), BF16)] * 6
        + [pltpu.VMEM((2, span, DH), F32)] * 4
        + [pltpu.VMEM((heads, DH, DH), F32)] * 3
        + [
            dma((heads, 3)),
            dma((heads, layer - 1, 3)),
            dma((heads, layer - 1, 3)),
            dma((heads, 2)),
            dma((heads, 2)),
            dma((heads,)),
            dma((heads,)),
            dma((heads,)),
            dma((heads, layer - 1)),
            dma((heads, layer - 1)),
        ],
        compiler_params=pltpu.CompilerParams(
            collective_id=0, has_side_effects=True, vmem_limit_bytes=56 * 2**20
        ),
    )(query_rows, key_rows, value_rows)


def solution(mesh):
    spec = P(("group", "seq"), None)
    return jax.shard_map(
        per_device, mesh=mesh, in_specs=(spec, spec, spec), out_specs=spec, check_vma=False
    )
```

```python
import functools
import math

import jax
import jax.numpy as jnp
from jax import lax
from jax.experimental import pallas as pl
from jax.experimental.pallas import tpu as pltpu
from jax.sharding import PartitionSpec as P

H = 16
DH = 128
WINDOW = 2048
TILE = 256
EPSILON = 1e-06
EXP_SCALE = math.log2(math.e) / math.sqrt(DH)
NEG = -1e30
SERVED = 1
LAG = 2
F32 = jnp.float32
BF16 = jnp.bfloat16
MESH = pl.DeviceIdType.MESH


def dot_nt(a, b):
    return lax.dot_general(a, b, (((1,), (1,)), ((), ())), preferred_element_type=F32)


def dot_tn(a, b):
    return lax.dot_general(a, b, (((0,), (0,)), ((), ())), preferred_element_type=F32)


def dot_nn(a, b):
    return jnp.dot(a, b, preferred_element_type=F32)


def times_state(q, state):
    high = state.astype(BF16)
    low = (state - high.astype(F32)).astype(BF16)
    both = dot_nn(q, jnp.concatenate([high, low], axis=1))
    return both[:, :DH] + both[:, DH:]


def head_norm(x):
    return x * lax.rsqrt(jnp.mean(x * x, axis=-1, keepdims=True) + EPSILON)


def kernel(
    layer, layers, rows,
    q_hbm, k_hbm, v_hbm, out_hbm,
    qb, kb, vb, kh, vh, ob, o_acc, m_acc, l_acc, lin_acc, total, state_in, state_out,
    q_back, o_serve, o_back, w_serve, w_back,
    own_sem, a_send, a_recv, z_send, z_recv, s_send, s_recv, o_own, o_send, o_recv,
    b_send, b_recv, f_send, f_recv,
):
    me = lax.axis_index("seq")
    place = lax.rem(me, layer)
    level = me // layer
    base = level * layer
    heads = H // layer
    served = min(SERVED, heads - 1)
    span = layer * rows
    tiles = span // TILE
    has_before = level > 0
    has_after = level < layers - 1

    pairs = layer // 2
    core, pair = lax.rem(place, 2), place // 2

    def toward(d):
        return lax.rem(pair + d // 2, pairs) * 2 + lax.rem(core + d % 2, 2)

    def origin(d):
        return lax.rem(pair + pairs - d // 2, pairs) * 2 + lax.rem(core + 2 - d % 2, 2)

    def peer(d):
        return base + toward(d)

    barrier = pltpu.get_barrier_semaphore()
    for d in range(1, layer):
        pl.semaphore_signal(barrier, inc=1, device_id={"seq": peer(d)}, device_id_type=MESH)

    @pl.when(has_before)
    def _():
        pl.semaphore_signal(barrier, inc=1, device_id={"seq": me - layer}, device_id_type=MESH)

    @pl.when(has_after)
    def _():
        pl.semaphore_signal(barrier, inc=1, device_id={"seq": me + layer}, device_id_type=MESH)

    ends = has_before.astype(jnp.int32) + has_after.astype(jnp.int32)
    pl.semaphore_wait(barrier, layer - 1 + ends)

    sources = (k_hbm, v_hbm, q_hbm)
    targets = (kb, vb, qb)

    def columns(owner, c):
        return pl.ds(pl.multiple_of((owner * heads + c) * DH, DH), DH)

    my_rows = pl.ds(pl.multiple_of(place * rows, rows), rows)

    def own_copy(c, t):
        return pltpu.make_async_copy(
            sources[t].at[:, columns(place, c)], targets[t].at[c, my_rows, :], own_sem.at[c, t]
        )

    def peer_copy(c, d, t):
        return pltpu.make_async_remote_copy(
            src_ref=sources[t].at[:, columns(toward(d), c)],
            dst_ref=targets[t].at[c, my_rows, :],
            send_sem=a_send.at[c, d - 1, t],
            recv_sem=a_recv.at[c, d - 1, t],
            device_id={"seq": peer(d)},
            device_id_type=MESH,
        )

    def next_copy(c, d, t):
        if d == 0:
            from_rows, source = my_rows, sources[t].at[:, columns(place, c)]
        else:
            from_rows = pl.ds(pl.multiple_of(origin(d) * rows, rows), rows)
            source = targets[t].at[c, from_rows, :]
        return pltpu.make_async_remote_copy(
            src_ref=source,
            dst_ref=(kh, vh)[t].at[c, from_rows, :],
            send_sem=z_send.at[c, d, t],
            recv_sem=z_recv.at[c, d, t],
            device_id={"seq": me + layer},
            device_id_type=MESH,
        )

    def back_copy(c):
        return pltpu.make_async_remote_copy(
            src_ref=qb.at[c],
            dst_ref=q_back.at[c],
            send_sem=b_send.at[c],
            recv_sem=b_recv.at[c],
            device_id={"seq": me - layer},
            device_id_type=MESH,
        )

    def served_copy(c, t):
        return pltpu.make_async_remote_copy(
            src_ref=(o_serve, w_serve)[t].at[c],
            dst_ref=(o_back, w_back)[t].at[c],
            send_sem=f_send.at[c, t],
            recv_sem=f_recv.at[c, t],
            device_id={"seq": me + layer},
            device_id_type=MESH,
        )

    def state_copy(c):
        return pltpu.make_async_remote_copy(
            src_ref=state_out.at[c],
            dst_ref=state_in.at[c],
            send_sem=s_send.at[c],
            recv_sem=s_recv.at[c],
            device_id={"seq": me + layer},
            device_id_type=MESH,
        )

    def out_copy(c, d):
        to_rows = pl.ds(pl.multiple_of(toward(d) * rows, rows), rows)
        return pltpu.make_async_remote_copy(
            src_ref=ob.at[c, to_rows, :],
            dst_ref=out_hbm.at[:, columns(place, c)],
            send_sem=o_send.at[c, d - 1],
            recv_sem=o_recv.at[c, d - 1],
            device_id={"seq": peer(d)},
            device_id_type=MESH,
        )

    def out_own(c):
        return pltpu.make_async_copy(
            ob.at[c, my_rows, :], out_hbm.at[:, columns(place, c)], o_own.at[c]
        )

    def send_near(c):
        for t in range(3):
            peer_copy(c, 1, t).start()
            own_copy(c, t).start()

    def send_far(c):
        for t in range(3):
            for d in range(2, layer):
                peer_copy(c, d, t).start()

    def wait_near(c):
        for t in range(2):
            peer_copy(c, 1, t).wait_recv()

    def pass_near(c):
        wait_near(c)

        @pl.when(has_after)
        def _():
            for d in range(2):
                for t in range(2):
                    next_copy(c, d, t).start()

    def wait_far(c):
        for t in range(2):
            for d in range(2, layer):
                peer_copy(c, d, t).wait_recv()

    def pass_far(c):
        @pl.when(has_after)
        def _():
            for d in range(2, layer):
                for t in range(2):
                    next_copy(c, d, t).start()

    def wait_rest(c):
        for t in range(3):
            own_copy(c, t).wait()
        for d in range(1, layer):
            peer_copy(c, d, 2).wait_recv()

    row_id = lax.broadcasted_iota(jnp.int32, (TILE, TILE), 0)
    col_id = lax.broadcasted_iota(jnp.int32, (TILE, TILE), 1)

    def part_softmax(q, k_full, v_full, s_diag, v_diag):
        peak = jnp.max(s_diag, axis=-1, keepdims=True)
        if k_full is not None:
            s_full = dot_nt(q, k_full)
            peak = jnp.maximum(peak, jnp.max(s_full, axis=-1, keepdims=True))
        p_diag = jnp.exp2((s_diag - peak) * EXP_SCALE)
        mass = jnp.sum(p_diag, axis=-1, keepdims=True)
        acc = dot_nn(p_diag.astype(BF16), v_diag)
        if k_full is not None:
            p_full = jnp.exp2((s_full - peak) * EXP_SCALE)
            mass = mass + jnp.sum(p_full, axis=-1, keepdims=True)
            acc = acc + dot_nn(p_full.astype(BF16), v_full)
        return peak, mass, acc

    def local_part(c, slot):
        causal = row_id >= col_id
        state = jnp.zeros((DH, DH), F32)
        for i in range(tiles):
            here = slice(i * TILE, (i + 1) * TILE)
            q, k, v = qb[c, here, :], kb[c, here, :], vb[c, here, :]
            scores = dot_nt(q, k)
            lin = dot_nn(jnp.where(causal, scores, 0.0).astype(BF16), v)
            if i > 0:
                lin = lin + times_state(q, state)
            lin_acc[slot, here, :] = lin
            state = state + dot_tn(k, v)
            k_full = kb[c, : i * TILE, :] if i > 0 else None
            v_full = vb[c, : i * TILE, :] if i > 0 else None
            peak, mass, acc = part_softmax(q, k_full, v_full, jnp.where(causal, scores, NEG), v)
            o_acc[slot, here, :] = acc
            m_acc[slot, here, :] = jnp.broadcast_to(peak, (TILE, DH))
            l_acc[slot, here, :] = jnp.broadcast_to(mass, (TILE, DH))
        total[c] = state

    def halo_tile(i, queries, keys, values, c):
        here = slice(i * TILE, (i + 1) * TILE)
        q, k, v = queries[c, here, :], keys[c, here, :], values[c, here, :]
        scores = jnp.where(col_id > row_id, dot_nt(q, k), NEG)
        k_full = keys[c, (i + 1) * TILE :, :] if i < tiles - 1 else None
        v_full = values[c, (i + 1) * TILE :, :] if i < tiles - 1 else None
        return part_softmax(q, k_full, v_full, scores, v)

    def halo_part(c, slot):
        state = state_in[c]
        for i in range(tiles):
            here = slice(i * TILE, (i + 1) * TILE)
            lin_acc[slot, here, :] += times_state(qb[c, here, :], state)
            peak, mass, acc = halo_tile(i, qb, kh, vh, c)
            before = m_acc[slot, here, :]
            both = jnp.maximum(before, peak)
            keep = jnp.exp2((before - both) * EXP_SCALE)
            take = jnp.exp2((peak - both) * EXP_SCALE)
            o_acc[slot, here, :] = o_acc[slot, here, :] * keep + acc * take
            l_acc[slot, here, :] = l_acc[slot, here, :] * keep + mass * take

    def serve(c):
        for i in range(tiles):
            here = slice(i * TILE, (i + 1) * TILE)
            peak, mass, acc = halo_tile(i, q_back, kb, vb, c)
            o_serve[c, here, :] = (acc / mass).astype(BF16)
            weight = jnp.broadcast_to(peak * EXP_SCALE + jnp.log2(mass), (TILE, DH))
            w_serve[c, :, here] = weight.T[:8, :]

    def merge_served(c, slot):
        state = state_in[c]
        for i in range(tiles):
            here = slice(i * TILE, (i + 1) * TILE)
            lin_acc[slot, here, :] += times_state(qb[c, here, :], state)
            weight = jnp.broadcast_to(w_back[c, 0:1, here], (DH, TILE)).T
            before = m_acc[slot, here, :] * EXP_SCALE
            both = jnp.maximum(before, weight)
            keep = jnp.exp2(before - both)
            take = jnp.exp2(weight - both)
            mean = o_back[c, here, :].astype(F32)
            o_acc[slot, here, :] = o_acc[slot, here, :] * keep + mean * take
            l_acc[slot, here, :] = l_acc[slot, here, :] * keep + take

    send_near(0)
    send_far(0)
    for c in range(1, heads):
        send_near(c)
    pass_near(served)

    def step(c, _):
        @pl.when(c < heads)
        def _():
            @pl.when(c < served)
            def _():
                wait_near(c)

            wait_far(c)

            @pl.when(c >= served)
            def _():
                pass_far(c)

            @pl.when(c + 1 < heads)
            def _():
                send_far(c + 1)

            @pl.when(c + 1 + served < heads)
            def _():
                pass_near(c + 1 + served)

            wait_rest(c)

            @pl.when(c < served)
            def _():
                @pl.when(has_before)
                def _():
                    back_copy(c).start()

            local_part(c, c)

        @pl.when(c > 0)
        def _():
            @pl.when(c <= served)
            def _():
                @pl.when(has_after)
                def _():
                    back_copy(c - 1).wait_recv()
                    serve(c - 1)
                    served_copy(c - 1, 0).start()
                    served_copy(c - 1, 1).start()

        @pl.when(c >= LAG)
        def _():
            h = c - LAG
            slot = h

            @pl.when(has_before)
            def _():
                state_copy(h).wait_recv()

            @pl.when(has_after)
            def _():
                @pl.when(has_before)
                def _():
                    state_out[h] = state_in[h] + total[h]

                @pl.when(level == 0)
                def _():
                    state_out[h] = total[h]

                state_copy(h).start()

            @pl.when(has_before)
            def _():
                @pl.when(h < served)
                def _():
                    served_copy(h, 0).wait_recv()
                    served_copy(h, 1).wait_recv()
                    merge_served(h, slot)

                @pl.when(h >= served)
                def _():
                    for d in range(layer):
                        for t in range(2):
                            next_copy(h, d, t).wait_recv()

                    halo_part(h, slot)

            def finish(i, _):
                here = pl.ds(pl.multiple_of(i * TILE, TILE), TILE)
                win = o_acc[slot, here, :] / l_acc[slot, here, :]
                ob[h, here, :] = (head_norm(lin_acc[slot, here, :]) + head_norm(win)).astype(BF16)
                return 0

            lax.fori_loop(0, tiles, finish, 0)
            for d in range(1, layer):
                out_copy(h, d).start()
            out_own(h).start()

        return 0

    lax.fori_loop(0, heads + LAG, step, 0)

    def drain(c, _):
        for d in range(1, layer):
            for t in range(3):
                peer_copy(c, d, t).wait_send()
            out_copy(c, d).wait_send()
            out_copy(c, d).wait_recv()
        out_own(c).wait()

        @pl.when(has_after)
        def _():
            @pl.when(c >= served)
            def _():
                for d in range(layer):
                    for t in range(2):
                        next_copy(c, d, t).wait_send()

            @pl.when(c < served)
            def _():
                served_copy(c, 0).wait_send()
                served_copy(c, 1).wait_send()

            state_copy(c).wait_send()

        @pl.when(has_before)
        def _():
            @pl.when(c < served)
            def _():
                back_copy(c).wait_send()

        return 0

    lax.fori_loop(0, heads, drain, 0)


def per_device(query_rows, key_rows, value_rows):
    rows = query_rows.shape[0]
    layer = WINDOW // rows
    layers = lax.axis_size("seq") // layer
    heads = H // layer
    span = layer * rows
    dma = pltpu.SemaphoreType.DMA
    return pl.pallas_call(
        functools.partial(kernel, layer, layers, rows),
        out_shape=jax.ShapeDtypeStruct(query_rows.shape, BF16),
        in_specs=[pl.BlockSpec(memory_space=pl.ANY)] * 3,
        out_specs=pl.BlockSpec(memory_space=pl.ANY),
        scratch_shapes=[pltpu.VMEM((heads, span, DH), BF16)] * 6
        + [pltpu.VMEM((heads, span, DH), F32)] * 4
        + [pltpu.VMEM((heads, DH, DH), F32)] * 3
        + [pltpu.VMEM((heads, span, DH), BF16)] * 3
        + [pltpu.VMEM((heads, 8, span), F32)] * 2
        + [
            dma((heads, 3)),
            dma((heads, layer - 1, 3)),
            dma((heads, layer - 1, 3)),
            dma((heads, layer, 2)),
            dma((heads, layer, 2)),
            dma((heads,)),
            dma((heads,)),
            dma((heads,)),
            dma((heads, layer - 1)),
            dma((heads, layer - 1)),
            dma((heads,)),
            dma((heads,)),
            dma((heads, 2)),
            dma((heads, 2)),
        ],
        compiler_params=pltpu.CompilerParams(
            collective_id=0, has_side_effects=True, vmem_limit_bytes=56 * 2**20
        ),
    )(query_rows, key_rows, value_rows)


def solution(mesh):
    spec = P(("group", "seq"), None)
    return jax.shard_map(
        per_device, mesh=mesh, in_specs=(spec, spec, spec), out_specs=spec, check_vma=False
    )
```

```python
import functools
import math

import jax
import jax.numpy as jnp
from jax import lax
from jax.experimental import pallas as pl
from jax.experimental.pallas import tpu as pltpu
from jax.sharding import PartitionSpec as P

H = 16
DH = 128
WINDOW = 2048
TILE = 256
EPSILON = 1e-06
EXP_SCALE = math.log2(math.e) / math.sqrt(DH)
NEG = -1e30
SERVED = 1
LAG = 2
F32 = jnp.float32
BF16 = jnp.bfloat16
MESH = pl.DeviceIdType.MESH


def dot_nt(a, b):
    return lax.dot_general(a, b, (((1,), (1,)), ((), ())), preferred_element_type=F32)


def dot_tn(a, b):
    return lax.dot_general(a, b, (((0,), (0,)), ((), ())), preferred_element_type=F32)


def dot_nn(a, b):
    return jnp.dot(a, b, preferred_element_type=F32)


def times_state(q, state):
    high = state.astype(BF16)
    low = (state - high.astype(F32)).astype(BF16)
    both = dot_nn(q, jnp.concatenate([high, low], axis=1))
    return both[:, :DH] + both[:, DH:]


def head_norm(x):
    return x * lax.rsqrt(jnp.mean(x * x, axis=-1, keepdims=True) + EPSILON)


def kernel(
    layer, layers, rows,
    q_hbm, k_hbm, v_hbm, out_hbm,
    qb, kb, vb, kh, vh, ob, o_acc, m_acc, l_acc, lin_acc, total, state_in, state_out,
    q_back, o_serve, o_back, w_serve, w_back,
    own_sem, a_send, a_recv, z_send, z_recv, s_send, s_recv, o_own, o_send, o_recv,
    b_send, b_recv, f_send, f_recv,
):
    me = lax.axis_index("seq")
    place = lax.rem(me, layer)
    level = me // layer
    base = level * layer
    heads = H // layer
    served = min(SERVED, heads - 1)
    span = layer * rows
    tiles = span // TILE
    has_before = level > 0
    has_after = level < layers - 1

    pairs = layer // 2
    core, pair = lax.rem(place, 2), place // 2

    def toward(d):
        return lax.rem(pair + d // 2, pairs) * 2 + lax.rem(core + d % 2, 2)

    def origin(d):
        return lax.rem(pair + pairs - d // 2, pairs) * 2 + lax.rem(core + 2 - d % 2, 2)

    def peer(d):
        return base + toward(d)

    barrier = pltpu.get_barrier_semaphore()
    for d in range(1, layer):
        pl.semaphore_signal(barrier, inc=1, device_id={"seq": peer(d)}, device_id_type=MESH)

    @pl.when(has_before)
    def _():
        pl.semaphore_signal(barrier, inc=1, device_id={"seq": me - layer}, device_id_type=MESH)

    @pl.when(has_after)
    def _():
        pl.semaphore_signal(barrier, inc=1, device_id={"seq": me + layer}, device_id_type=MESH)

    ends = has_before.astype(jnp.int32) + has_after.astype(jnp.int32)
    pl.semaphore_wait(barrier, layer - 1 + ends)

    sources = (k_hbm, v_hbm, q_hbm)
    targets = (kb, vb, qb)

    def columns(owner, c):
        return pl.ds(pl.multiple_of((owner * heads + c) * DH, DH), DH)

    my_rows = pl.ds(pl.multiple_of(place * rows, rows), rows)

    def own_copy(c, t):
        return pltpu.make_async_copy(
            sources[t].at[:, columns(place, c)], targets[t].at[c, my_rows, :], own_sem.at[c, t]
        )

    def peer_copy(c, d, t):
        return pltpu.make_async_remote_copy(
            src_ref=sources[t].at[:, columns(toward(d), c)],
            dst_ref=targets[t].at[c, my_rows, :],
            send_sem=a_send.at[c, d - 1, t],
            recv_sem=a_recv.at[c, d - 1, t],
            device_id={"seq": peer(d)},
            device_id_type=MESH,
        )

    def next_copy(c, d, t):
        if d == 0:
            from_rows, source = my_rows, sources[t].at[:, columns(place, c)]
        else:
            from_rows = pl.ds(pl.multiple_of(origin(d) * rows, rows), rows)
            source = targets[t].at[c, from_rows, :]
        return pltpu.make_async_remote_copy(
            src_ref=source,
            dst_ref=(kh, vh)[t].at[c, from_rows, :],
            send_sem=z_send.at[c, d, t],
            recv_sem=z_recv.at[c, d, t],
            device_id={"seq": me + layer},
            device_id_type=MESH,
        )

    def back_copy(c):
        return pltpu.make_async_remote_copy(
            src_ref=qb.at[c],
            dst_ref=q_back.at[c],
            send_sem=b_send.at[c],
            recv_sem=b_recv.at[c],
            device_id={"seq": me - layer},
            device_id_type=MESH,
        )

    def served_copy(c, t):
        return pltpu.make_async_remote_copy(
            src_ref=(o_serve, w_serve)[t].at[c],
            dst_ref=(o_back, w_back)[t].at[c],
            send_sem=f_send.at[c, t],
            recv_sem=f_recv.at[c, t],
            device_id={"seq": me + layer},
            device_id_type=MESH,
        )

    def state_copy(c):
        return pltpu.make_async_remote_copy(
            src_ref=state_out.at[c],
            dst_ref=state_in.at[c],
            send_sem=s_send.at[c],
            recv_sem=s_recv.at[c],
            device_id={"seq": me + layer},
            device_id_type=MESH,
        )

    def out_copy(c, d):
        to_rows = pl.ds(pl.multiple_of(toward(d) * rows, rows), rows)
        return pltpu.make_async_remote_copy(
            src_ref=ob.at[c, to_rows, :],
            dst_ref=out_hbm.at[:, columns(place, c)],
            send_sem=o_send.at[c, d - 1],
            recv_sem=o_recv.at[c, d - 1],
            device_id={"seq": peer(d)},
            device_id_type=MESH,
        )

    def out_own(c):
        return pltpu.make_async_copy(
            ob.at[c, my_rows, :], out_hbm.at[:, columns(place, c)], o_own.at[c]
        )

    def send_near(c):
        for t in range(3):
            peer_copy(c, 1, t).start()
            own_copy(c, t).start()

    def send_far(c):
        for t in range(3):
            for d in range(2, layer):
                peer_copy(c, d, t).start()

    def wait_near(c):
        for t in range(2):
            peer_copy(c, 1, t).wait_recv()

    def pass_near(c):
        wait_near(c)

        @pl.when(has_after)
        def _():
            for d in range(2):
                for t in range(2):
                    next_copy(c, d, t).start()

    def wait_far(c):
        for t in range(2):
            for d in range(2, layer):
                peer_copy(c, d, t).wait_recv()

    def pass_far(c):
        @pl.when(has_after)
        def _():
            for d in range(2, layer):
                for t in range(2):
                    next_copy(c, d, t).start()

    def wait_rest(c):
        for t in range(3):
            own_copy(c, t).wait()
        for d in range(1, layer):
            peer_copy(c, d, 2).wait_recv()

    row_id = lax.broadcasted_iota(jnp.int32, (TILE, TILE), 0)
    col_id = lax.broadcasted_iota(jnp.int32, (TILE, TILE), 1)

    def part_softmax(q, k_full, v_full, s_diag, v_diag):
        peak = jnp.max(s_diag, axis=-1, keepdims=True)
        if k_full is not None:
            s_full = dot_nt(q, k_full)
            peak = jnp.maximum(peak, jnp.max(s_full, axis=-1, keepdims=True))
        p_diag = jnp.exp2((s_diag - peak) * EXP_SCALE)
        mass = jnp.sum(p_diag, axis=-1, keepdims=True)
        acc = dot_nn(p_diag.astype(BF16), v_diag)
        if k_full is not None:
            p_full = jnp.exp2((s_full - peak) * EXP_SCALE)
            mass = mass + jnp.sum(p_full, axis=-1, keepdims=True)
            acc = acc + dot_nn(p_full.astype(BF16), v_full)
        return peak, mass, acc

    def local_part(c, slot):
        causal = row_id >= col_id
        state = jnp.zeros((DH, DH), F32)
        for i in range(tiles):
            here = slice(i * TILE, (i + 1) * TILE)
            q, k, v = qb[c, here, :], kb[c, here, :], vb[c, here, :]
            scores = dot_nt(q, k)
            lin = dot_nn(jnp.where(causal, scores, 0.0).astype(BF16), v)
            if i > 0:
                lin = lin + times_state(q, state)
            lin_acc[slot, here, :] = lin
            state = state + dot_tn(k, v)
            k_full = kb[c, : i * TILE, :] if i > 0 else None
            v_full = vb[c, : i * TILE, :] if i > 0 else None
            peak, mass, acc = part_softmax(q, k_full, v_full, jnp.where(causal, scores, NEG), v)
            o_acc[slot, here, :] = acc
            m_acc[slot, here, :] = jnp.broadcast_to(peak, (TILE, DH))
            l_acc[slot, here, :] = jnp.broadcast_to(mass, (TILE, DH))
        total[c] = state

    def halo_tile(i, queries, keys, values, c):
        here = slice(i * TILE, (i + 1) * TILE)
        q, k, v = queries[c, here, :], keys[c, here, :], values[c, here, :]
        scores = jnp.where(col_id > row_id, dot_nt(q, k), NEG)
        k_full = keys[c, (i + 1) * TILE :, :] if i < tiles - 1 else None
        v_full = values[c, (i + 1) * TILE :, :] if i < tiles - 1 else None
        return part_softmax(q, k_full, v_full, scores, v)

    def finish(c, slot, r):
        here = slice(r * rows, (r + 1) * rows)
        win = o_acc[slot, here, :] / l_acc[slot, here, :]
        ob[c, here, :] = (head_norm(lin_acc[slot, here, :]) + head_norm(win)).astype(BF16)
        for d in range(1, layer):
            @pl.when(toward(d) == r)
            def _():
                out_copy(c, d).start()

        @pl.when(place == r)
        def _():
            out_own(c).start()

    def halo_part(c, slot):
        state = state_in[c]
        for i in range(tiles):
            here = slice(i * TILE, (i + 1) * TILE)
            lin_acc[slot, here, :] += times_state(qb[c, here, :], state)
            peak, mass, acc = halo_tile(i, qb, kh, vh, c)
            before = m_acc[slot, here, :]
            both = jnp.maximum(before, peak)
            keep = jnp.exp2((before - both) * EXP_SCALE)
            take = jnp.exp2((peak - both) * EXP_SCALE)
            o_acc[slot, here, :] = o_acc[slot, here, :] * keep + acc * take
            l_acc[slot, here, :] = l_acc[slot, here, :] * keep + mass * take
            if (i + 1) * TILE % rows == 0:
                finish(c, slot, i // (rows // TILE))

    def serve(c):
        for i in range(tiles):
            here = slice(i * TILE, (i + 1) * TILE)
            peak, mass, acc = halo_tile(i, q_back, kb, vb, c)
            o_serve[c, here, :] = (acc / mass).astype(BF16)
            weight = jnp.broadcast_to(peak * EXP_SCALE + jnp.log2(mass), (TILE, DH))
            w_serve[c, :, here] = weight.T[:8, :]

    def merge_served(c, slot):
        state = state_in[c]
        for i in range(tiles):
            here = slice(i * TILE, (i + 1) * TILE)
            lin_acc[slot, here, :] += times_state(qb[c, here, :], state)
            weight = jnp.broadcast_to(w_back[c, 0:1, here], (DH, TILE)).T
            before = m_acc[slot, here, :] * EXP_SCALE
            both = jnp.maximum(before, weight)
            keep = jnp.exp2(before - both)
            take = jnp.exp2(weight - both)
            mean = o_back[c, here, :].astype(F32)
            o_acc[slot, here, :] = o_acc[slot, here, :] * keep + mean * take
            l_acc[slot, here, :] = l_acc[slot, here, :] * keep + take
            if (i + 1) * TILE % rows == 0:
                finish(c, slot, i // (rows // TILE))

    send_near(0)
    send_far(0)
    for c in range(1, heads):
        send_near(c)
    pass_near(served)

    def step(c, _):
        @pl.when(c < heads)
        def _():
            @pl.when(c < served)
            def _():
                wait_near(c)

            wait_far(c)

            @pl.when(c >= served)
            def _():
                pass_far(c)

            @pl.when(c + 1 < heads)
            def _():
                send_far(c + 1)

            @pl.when(c + 1 + served < heads)
            def _():
                pass_near(c + 1 + served)

            wait_rest(c)

            @pl.when(c < served)
            def _():
                @pl.when(has_before)
                def _():
                    back_copy(c).start()

            local_part(c, c)

        @pl.when(c > 0)
        def _():
            @pl.when(c <= served)
            def _():
                @pl.when(has_after)
                def _():
                    back_copy(c - 1).wait_recv()
                    serve(c - 1)
                    served_copy(c - 1, 0).start()
                    served_copy(c - 1, 1).start()

        @pl.when(c >= LAG)
        def _():
            h = c - LAG
            slot = h

            @pl.when(has_before)
            def _():
                state_copy(h).wait_recv()

            @pl.when(has_after)
            def _():
                @pl.when(has_before)
                def _():
                    state_out[h] = state_in[h] + total[h]

                @pl.when(level == 0)
                def _():
                    state_out[h] = total[h]

                state_copy(h).start()

            @pl.when(has_before)
            def _():
                @pl.when(h < served)
                def _():
                    served_copy(h, 0).wait_recv()
                    served_copy(h, 1).wait_recv()
                    merge_served(h, slot)

                @pl.when(h >= served)
                def _():
                    for d in range(layer):
                        for t in range(2):
                            next_copy(h, d, t).wait_recv()

                    halo_part(h, slot)

            @pl.when(level == 0)
            def _():
                for r in range(layer):
                    finish(h, slot, r)

        return 0

    lax.fori_loop(0, heads + LAG, step, 0)

    def drain(c, _):
        for d in range(1, layer):
            for t in range(3):
                peer_copy(c, d, t).wait_send()
            out_copy(c, d).wait_send()
            out_copy(c, d).wait_recv()
        out_own(c).wait()

        @pl.when(has_after)
        def _():
            @pl.when(c >= served)
            def _():
                for d in range(layer):
                    for t in range(2):
                        next_copy(c, d, t).wait_send()

            @pl.when(c < served)
            def _():
                served_copy(c, 0).wait_send()
                served_copy(c, 1).wait_send()

            state_copy(c).wait_send()

        @pl.when(has_before)
        def _():
            @pl.when(c < served)
            def _():
                back_copy(c).wait_send()

        return 0

    lax.fori_loop(0, heads, drain, 0)


def per_device(query_rows, key_rows, value_rows):
    rows = query_rows.shape[0]
    layer = WINDOW // rows
    layers = lax.axis_size("seq") // layer
    heads = H // layer
    span = layer * rows
    dma = pltpu.SemaphoreType.DMA
    return pl.pallas_call(
        functools.partial(kernel, layer, layers, rows),
        out_shape=jax.ShapeDtypeStruct(query_rows.shape, BF16),
        in_specs=[pl.BlockSpec(memory_space=pl.ANY)] * 3,
        out_specs=pl.BlockSpec(memory_space=pl.ANY),
        scratch_shapes=[pltpu.VMEM((heads, span, DH), BF16)] * 6
        + [pltpu.VMEM((heads, span, DH), F32)] * 4
        + [pltpu.VMEM((heads, DH, DH), F32)] * 3
        + [pltpu.VMEM((heads, span, DH), BF16)] * 3
        + [pltpu.VMEM((heads, 8, span), F32)] * 2
        + [
            dma((heads, 3)),
            dma((heads, layer - 1, 3)),
            dma((heads, layer - 1, 3)),
            dma((heads, layer, 2)),
            dma((heads, layer, 2)),
            dma((heads,)),
            dma((heads,)),
            dma((heads,)),
            dma((heads, layer - 1)),
            dma((heads, layer - 1)),
            dma((heads,)),
            dma((heads,)),
            dma((heads, 2)),
            dma((heads, 2)),
        ],
        compiler_params=pltpu.CompilerParams(
            collective_id=0, has_side_effects=True, vmem_limit_bytes=56 * 2**20
        ),
    )(query_rows, key_rows, value_rows)


def solution(mesh):
    spec = P(("group", "seq"), None)
    return jax.shard_map(
        per_device, mesh=mesh, in_specs=(spec, spec, spec), out_specs=spec, check_vma=False
    )
```
